256 devices in a mesh: ta: 16 (over x_hi, z), ha: 16 (over y, x_lo, core).
Axes of the slice: x: 4 (x_hi: 2, x_lo: 2; x = x_hi * 2 + x_lo), y: 4, z: 8, core: 2. Of those that a mesh axis runs over, the one named last changes fastest.
Arguments:
- queries: bfloat16 [16, 64, 32, 1280], P('ta', 'ha'), may hold values from -6 to 6
- keys: bfloat16 [16, 64, 32, 1280], P('ta', 'ha'), may hold values from -6 to 6
- values: bfloat16 [16, 64, 32, 1280], P('ta', 'ha'), may hold values from -6 to 6
- grad_out: bfloat16 [16, 64, 32, 2560], P('ta', 'ha'), may hold values from -6 to 6
- out_weight: bfloat16 [1280, 2560], P(('ta', 'ha')), may hold values from -0.15625 to 0.15625
- windows: int32 [16, 64, 4, 3], P('ta', 'ha'), may hold values from 0 to 1
Outputs:
- grad_query: bfloat16 [16, 64, 32, 1280], P('ta', 'ha')
- grad_key: bfloat16 [16, 64, 32, 1280], P('ta', 'ha')
- grad_value: bfloat16 [16, 64, 32, 1280], P('ta', 'ha')
- weight_grad: float32 [1280, 2560], P(('ta', 'ha'))
The draws below stay inside these ranges and needn't reach their ends.
All inputs are finite; a program needn't handle non-finite values.
Results may differ from the reference program's by a relative error of at most 0.024.
Values may be sent and summed in bfloat16 or wider, within the bound.
No kernel may reach another device: no remote copies, remote signals or barrier semaphores. Data moves between devices by JAX's collectives and lax.ppermute only.
A program may use at most 128 MiB of HBM per device.

```python
import jax
import jax.numpy as jnp
from jax import lax

D = 2560
HEADS = 20
HEAD_DIM = 64
HD = 1280
TILE_W = 8
NW = 32
CH = 4
NT = 16
NH = 64
NWT = 4
N_TA = 16
N_HA = 16


def draw_queries(key, part):
    base = jnp.clip(jax.random.normal(jax.random.fold_in(key, 1), (NT, NH, NW, HD), jnp.float32), -6.0, 6.0)
    return base.astype(jnp.bfloat16)


def draw_keys(key, part):
    base = jnp.clip(jax.random.normal(jax.random.fold_in(key, 2), (NT, NH, NW, HD), jnp.float32), -6.0, 6.0)
    return base.astype(jnp.bfloat16)


def plant(values, key, smallest, top_value):
    longest = values.shape.index(max(values.shape))
    spots = []
    for shift in (0, 1):
        where = [jax.random.randint(jax.random.fold_in(key, axis), (), 0, length) for axis, length in enumerate(values.shape)]
        where[longest] = (where[longest] + shift) % values.shape[longest]
        spots.append(tuple(where))
    return values.at[spots[0]].set(smallest).at[spots[1]].set(top_value)


def levels(own_key, shape, cuts, low, top_value):
    loudness, own = 1.0, jax.random.fold_in(own_key, 6)
    for dim, shards_of in cuts:
        draws = jnp.exp(jax.random.uniform(jax.random.fold_in(own, dim), (shards_of,), jnp.float32, low / len(cuts), top_value / len(cuts)))
        loudness = loudness * jnp.repeat(draws, shape[dim] // shards_of).reshape([-1 if axis == dim else 1 for axis in range(len(shape))])
    return loudness


def normal_values(stream_key, shape, scale, most, shards=(), kind=jnp.bfloat16):
    array = jax.random.normal(stream_key, shape, jnp.float32) * scale
    if len(shards) > 0:
        array = levels(stream_key, shape, shards, -0.22, 0.18) * array
    return jnp.clip(array, min=-most, max=most).astype(kind)


def setup_inputs(seed: int = 0) -> dict:
    key_of = jax.random.split(jax.random.key(seed), 7)
    return {
        "queries": draw_queries(jax.random.fold_in(key_of[6], 71), 0),
        "keys": draw_keys(jax.random.fold_in(key_of[6], 71), 0),
        "values": normal_values(key_of[2], (NT, NH, NW, HD), 1.0, 6.0, ((0, 16), (1, 16))),
        "grad_out": normal_values(key_of[3], (NT, NH, NW, D), 1.0, 6.0, ((0, 16), (1, 16))),
        "out_weight": normal_values(key_of[4], (HD, D), HD ** -0.5, 0.15625, ((0, 256),)),
        "windows": plant(jax.random.randint(key_of[5], (NT, NH, NWT, 3), 0, 2), jax.random.fold_in(key_of[5], 1), 0, 1).astype(jnp.int32),
    }


def rounded(tensor):
    return lax.optimization_barrier(tensor.astype(jnp.bfloat16)).astype(jnp.float32)


def grid_positions(first_time, first_row, frames, row_count, col_count):
    grid_shape = (frames, row_count, col_count)
    time_index = first_time + lax.broadcasted_iota(jnp.int32, grid_shape, 0)
    row_index = first_row + lax.broadcasted_iota(jnp.int32, grid_shape, 1)
    tile_index = lax.broadcasted_iota(jnp.int32, grid_shape, 2) // TILE_W
    return jnp.stack([time_index, row_index, tile_index], axis=-1)


def visible(query_pos, query_ext, query_valid, key_pos, key_valid):
    distance = jnp.abs(query_pos[:, None, :] - key_pos[None, :, :])
    inside = jnp.all(distance <= query_ext[:, None, :], axis=2)
    return inside & query_valid[:, None] & key_valid[None, :]


def by_heads(tensor):
    return tensor.astype(jnp.float32).reshape(tensor.shape[0], HEADS, HEAD_DIM).transpose(1, 0, 2)


def masked_scores(query_heads, key_heads, allowed):
    raw_scores = jnp.einsum("hqd,hkd->hqk", query_heads, key_heads) * HEAD_DIM ** -0.5
    return jnp.where(allowed[None], raw_scores, -1e30)


def forward_block(block_queries, block_keys, block_values, allowed):
    scores = masked_scores(by_heads(block_queries), by_heads(block_keys), allowed)
    row_max = jnp.max(scores, axis=2, keepdims=True)
    row_total = jnp.sum(jnp.where(allowed[None], jnp.exp(scores - row_max), 0.0), axis=2, keepdims=True)
    log_total = row_max + jnp.log(row_total)
    attention = rounded(jnp.where(allowed[None], jnp.exp(scores - log_total), 0.0))
    combined = jnp.einsum("hqk,hkd->qhd", attention, by_heads(block_values))
    return combined.reshape(combined.shape[0], -1).astype(jnp.bfloat16), log_total[..., 0].T


def backward_block(block_queries, block_grads, block_total, block_delta, block_keys, block_values, allowed):
    query_heads = by_heads(block_queries)
    grad_heads = by_heads(block_grads)
    key_heads = by_heads(block_keys)
    value_heads = by_heads(block_values)
    scores = masked_scores(query_heads, key_heads, allowed)
    recomputed = jnp.where(allowed[None], jnp.exp(scores - block_total.T[:, :, None]), 0.0)
    value_grad = jnp.einsum("hqk,hqd->khd", rounded(recomputed), grad_heads)
    score_grad = jnp.einsum("hqd,hkd->hqk", grad_heads, value_heads)
    rounded_grad = rounded(recomputed * (score_grad - block_delta.T[:, :, None]))
    query_grad = jnp.einsum("hqk,hkd->qhd", rounded_grad, key_heads) * HEAD_DIM ** -0.5
    key_grad = jnp.einsum("hqk,hqd->khd", rounded_grad, query_heads) * HEAD_DIM ** -0.5
    return (query_grad.reshape(query_grad.shape[0], -1), key_grad.reshape(key_grad.shape[0], -1),
            value_grad.reshape(value_grad.shape[0], -1))


def reference(queries, keys, values, grad_out, out_weight, windows):
    frames, all_rows, col_count, inner = queries.shape
    model_width = grad_out.shape[3]
    token_count = frames * all_rows * col_count
    flat_grad = grad_out.reshape(token_count, model_width)
    grad_attn = jnp.dot(flat_grad, out_weight.T, preferred_element_type=jnp.float32).astype(jnp.bfloat16)
    grad_attn = lax.optimization_barrier(grad_attn).reshape(frames, all_rows, col_count, inner)
    padding = ((1, 1), (1, 1), (0, 0), (0, 0))
    padded_queries = jnp.pad(queries, padding)
    padded_keys = jnp.pad(keys, padding)
    padded_values = jnp.pad(values, padding)
    padded_grad = jnp.pad(grad_attn, padding)
    positions = grid_positions(-1, -1, frames + 2, all_rows + 2, col_count)
    inside_grid = ((positions[..., 0] >= 0) & (positions[..., 0] < frames)
                   & (positions[..., 1] >= 0) & (positions[..., 1] < all_rows))
    extents = jnp.pad(jnp.repeat(windows, TILE_W, axis=2), padding)
    zero = jnp.zeros((), jnp.int32)

    def own(tensor, time_block, row_block):
        starts = (time_block + 1, row_block * CH + 1) + (zero,) * (tensor.ndim - 2)
        piece = lax.dynamic_slice(tensor, starts, (1, CH) + tensor.shape[2:])
        return piece.reshape((-1,) + tensor.shape[3:])

    def nearby(tensor, time_block, row_block):
        starts = (time_block, row_block * CH) + (zero,) * (tensor.ndim - 2)
        piece = lax.dynamic_slice(tensor, starts, (3, CH + 2) + tensor.shape[2:])
        return piece.reshape((-1,) + tensor.shape[3:])

    def one_block(carry, block):
        key_sums, value_sums = carry
        time_block = block // N_HA
        row_block = block % N_HA
        allowed = visible(own(positions, time_block, row_block), own(extents, time_block, row_block),
                          own(inside_grid, time_block, row_block), nearby(positions, time_block, row_block),
                          nearby(inside_grid, time_block, row_block))
        block_queries = own(padded_queries, time_block, row_block)
        block_keys = nearby(padded_keys, time_block, row_block)
        block_values = nearby(padded_values, time_block, row_block)
        attended, log_total = forward_block(block_queries, block_keys, block_values, allowed)
        attended = lax.optimization_barrier(attended)
        block_grad = own(padded_grad, time_block, row_block)
        row_delta = jnp.sum((block_grad.astype(jnp.float32) * attended.astype(jnp.float32))
                            .reshape(-1, HEADS, HEAD_DIM), axis=2)
        query_grad, key_grad, value_grad = backward_block(block_queries, block_grad, log_total, row_delta,
                                                          block_keys, block_values, allowed)
        starts = (time_block, row_block * CH, zero, zero)
        sizes = (3, CH + 2, col_count, inner)
        key_sums = lax.dynamic_update_slice(
            key_sums, lax.dynamic_slice(key_sums, starts, sizes) + key_grad.reshape(sizes), starts)
        value_sums = lax.dynamic_update_slice(
            value_sums, lax.dynamic_slice(value_sums, starts, sizes) + value_grad.reshape(sizes), starts)
        return (key_sums, value_sums), (attended, query_grad.astype(jnp.bfloat16))

    empty = jnp.zeros((frames + 2, all_rows + 2, col_count, inner), jnp.float32)
    blocks = jnp.arange(N_TA * N_HA, dtype=jnp.int32)
    (key_sums, value_sums), (attended, query_grad) = lax.scan(one_block, (empty, empty), blocks)
    weight_grad = jnp.dot(attended.reshape(token_count, inner).T, flat_grad,
                          preferred_element_type=jnp.float32) * token_count ** -0.5
    out_shape = (frames, all_rows, col_count, inner)
    return (query_grad.reshape(out_shape), key_sums[1:-1, 1:-1].astype(jnp.bfloat16),
            value_sums[1:-1, 1:-1].astype(jnp.bfloat16), weight_grad)
```

```python
import jax
import jax.numpy as jnp
from jax import lax
from jax.experimental import pallas as pl
from jax.experimental.pallas import tpu as pltpu
from jax.sharding import PartitionSpec as P

HEAD_DIM = 64
TILE_W = 8
LANES = 128
SIZES = {"x": 4, "y": 4, "z": 8, "c": 2}
BOTH = ("ta", "ha")
NEG = -1e30


def device_number(x, y, z, c):
    return ((x // 2) * 8 + z) * 16 + y * 4 + (x % 2) * 2 + c


def moved(value, dim, steps):
    pairs = []
    for x in range(4):
        for y in range(4):
            for z in range(8):
                for c in range(2):
                    at = {"x": x, "y": y, "z": z, "c": c}
                    to = dict(at)
                    to[dim] = (at[dim] + steps) % SIZES[dim]
                    pairs.append((device_number(**at), device_number(**to)))
    return lax.ppermute(value, BOTH, pairs)


def shifted(value, axis, steps):
    count = lax.axis_size(axis)
    first, last = (max(0, -steps), min(count, count - steps))
    return lax.ppermute(value, axis, [(source, source + steps) for source in range(first, last)])


def ahead(value, dim):
    return [value] + [moved(value, dim, -k) for k in range(1, SIZES[dim])]


def summed(pieces, dim):
    total = pieces[0].astype(jnp.float32)
    for k in range(1, SIZES[dim]):
        total = total + moved(pieces[k], dim, k).astype(jnp.float32)
    return total


def gathered_weight(weight):
    half = weight.shape[1] // 2
    rows = jnp.concatenate(ahead(weight, "z"), axis=0)
    n = rows.shape[0]
    first = jnp.concatenate(ahead(rows[:, :half], "x"), axis=0)
    second = jnp.concatenate(ahead(rows[:, half:], "y"), axis=0)
    first = jnp.concatenate(ahead(first, "y"), axis=0)
    pieces = [p.reshape(4, n, half) for p in ahead(second, "x")]
    second = jnp.stack(pieces, axis=1).reshape(16 * n, half)
    return first, second


def scattered_sum(partial):
    rows, width = partial.shape
    half = width // 2
    n = rows // 16
    first = partial[:, :half].reshape(4, 4 * n, half)
    second = partial[:, half:].reshape(4, 4, n, half)
    first = summed([first[k] for k in range(4)], "y").astype(jnp.bfloat16).reshape(4, n, half)
    second = summed([second[:, k] for k in range(4)], "x").astype(jnp.bfloat16)
    first = summed([first[k] for k in range(4)], "x").astype(jnp.bfloat16)
    second = summed([second[k] for k in range(4)], "y").astype(jnp.bfloat16)
    both = jnp.concatenate([first, second], axis=1).reshape(8, n // 8, width)
    return summed([both[k] for k in range(8)], "z")


def row_order(own_rows):
    ta = lax.axis_index("ta")
    ha = lax.axis_index("ha")
    x = (ta // 8) * 2 + (ha // 2) % 2
    y = ha // 4
    z = ta % 8
    c = ha % 2
    shape = (2, 4, 4, 8, own_rows)
    core = (c + lax.broadcasted_iota(jnp.int32, shape, 0)) % 2
    at_y = (y + lax.broadcasted_iota(jnp.int32, shape, 1)) % 4
    at_x = (x + lax.broadcasted_iota(jnp.int32, shape, 2)) % 4
    at_z = (z + lax.broadcasted_iota(jnp.int32, shape, 3)) % 8
    row = lax.broadcasted_iota(jnp.int32, shape, 4)
    number = ((at_x // 2) * 8 + at_z) * 16 + at_y * 4 + (at_x % 2) * 2 + core
    return (number * own_rows + row).reshape(-1)


def visible_keys(windows, frames_in_all, rows_in_all, row_count, col_count):
    time_index = lax.axis_index("ta")
    first_row = lax.axis_index("ha") * row_count
    extent = jnp.repeat(windows[0], TILE_W, axis=1).reshape(row_count * col_count, 3)
    shape = (3, row_count + 2, col_count, row_count, col_count)
    key_frame = lax.broadcasted_iota(jnp.int32, shape, 0) - 1
    key_row = lax.broadcasted_iota(jnp.int32, shape, 1) - 1
    key_tile = lax.broadcasted_iota(jnp.int32, shape, 2) // TILE_W
    query_row = lax.broadcasted_iota(jnp.int32, shape, 3)
    query_tile = lax.broadcasted_iota(jnp.int32, shape, 4) // TILE_W
    flat = (3 * (row_count + 2) * col_count, row_count * col_count)
    apart = [jnp.abs(key_frame), jnp.abs(key_row - query_row), jnp.abs(key_tile - query_tile)]
    inside = (
        (key_frame + time_index >= 0)
        & (key_frame + time_index < frames_in_all)
        & (key_row + first_row >= 0)
        & (key_row + first_row < rows_in_all)
    ).reshape(flat)
    for axis in range(3):
        inside = inside & (apart[axis].reshape(flat) <= extent[None, :, axis])
    return jnp.where(inside, 0.0, NEG).astype(jnp.float32)


def stacked(pair):
    lane = lax.broadcasted_iota(jnp.int32, pair.shape, 1)
    zero = jnp.zeros_like(pair)
    return jnp.concatenate(
        [jnp.where(lane < HEAD_DIM, pair, zero), jnp.where(lane < HEAD_DIM, zero, pair)], axis=0
    )


def unstacked(both):
    n = both.shape[0] // 2
    lane = lax.broadcasted_iota(jnp.int32, (n, LANES), 1)
    return jnp.where(lane < HEAD_DIM, both[:n], both[n:])


def dot(a, b, a_dim, b_dim):
    return lax.dot_general(
        a, b, (((a_dim,), (b_dim,)), ((), ())), preferred_element_type=jnp.float32
    )


def near(refs, which):
    return jnp.concatenate([ref[which] for ref in refs], axis=0)


def attend_kernel(q_ref, prev_ref, own_ref, next_ref, bias_ref, out_ref, total_ref):
    refs = (prev_ref, own_ref, next_ref)
    queries = stacked(q_ref[...] * jnp.asarray(HEAD_DIM**-0.5, jnp.bfloat16))
    scores = dot(near(refs, 0), queries, 1, 1)
    bias = bias_ref[...]
    scores = scores + jnp.concatenate([bias, bias], axis=1)
    top = jnp.max(scores, axis=0, keepdims=True)
    raised = jnp.exp(scores - top)
    total = jnp.sum(raised, axis=0, keepdims=True)
    total_ref[...] = jnp.broadcast_to(top + jnp.log(total), total_ref.shape)
    mixed = dot(near(refs, 1), raised.astype(jnp.bfloat16), 0, 0) / total
    out_ref[...] = unstacked(mixed.T).astype(jnp.bfloat16)


def grads_kernel(
    q_ref, g_ref, total_ref, prev_ref, own_ref, next_ref, bias_ref,
    dq_ref, dprev_ref, down_ref, dnext_ref,
):
    refs = (prev_ref, own_ref, next_ref)
    queries = stacked(q_ref[...] * jnp.asarray(HEAD_DIM**-0.5, jnp.bfloat16))
    grads = stacked(g_ref[...])
    keys = near(refs, 0)
    bias = bias_ref[...]
    scores = dot(keys, queries, 1, 1) + jnp.concatenate([bias, bias], axis=1)
    weights = jnp.exp(scores - total_ref[0:1, :])
    dweights = weights * dot(near(refs, 1), grads, 1, 1)
    delta = jnp.sum(dweights, axis=0, keepdims=True)
    dscores = (dweights - weights * delta).astype(jnp.bfloat16)
    dvalues = dot(weights.astype(jnp.bfloat16), grads, 1, 0)
    dkeys = dot(dscores, queries, 1, 0)
    dqueries = dot(keys, dscores, 0, 0) * HEAD_DIM**-0.5
    dq_ref[...] = unstacked(dqueries.T).astype(jnp.bfloat16)
    n = dprev_ref.shape[1]
    for i, ref in enumerate((dprev_ref, down_ref, dnext_ref)):
        ref[0] = dkeys[i * n : (i + 1) * n].astype(jnp.bfloat16)
        ref[1] = dvalues[i * n : (i + 1) * n].astype(jnp.bfloat16)


def attend(queries, nearby, bias):
    tokens, inner = queries.shape
    keys = nearby[0].shape[1]
    pairs = inner // LANES
    by_pair = pl.BlockSpec((tokens, LANES), lambda j: (0, j))
    near_spec = pl.BlockSpec((2, keys, LANES), lambda j: (0, 0, j))
    return pl.pallas_call(
        attend_kernel,
        grid=(pairs,),
        in_specs=[by_pair, near_spec, near_spec, near_spec,
                  pl.BlockSpec(bias.shape, lambda j: (0, 0))],
        out_specs=[by_pair, pl.BlockSpec((None, 8, 2 * tokens), lambda j: (j, 0, 0))],
        out_shape=[
            jax.ShapeDtypeStruct((tokens, inner), jnp.bfloat16),
            jax.ShapeDtypeStruct((pairs, 8, 2 * tokens), jnp.float32),
        ],
        cost_estimate=pl.CostEstimate(
            flops=4 * 3 * keys * tokens * inner * 2, bytes_accessed=6 * keys * inner * 2,
            transcendentals=3 * keys * tokens * 20),
        name="attend",
    )(queries, *nearby, bias)


def attention_grads(queries, grads, totals, nearby, bias):
    tokens, inner = queries.shape
    keys = nearby[0].shape[1]
    pairs = inner // LANES
    by_pair = pl.BlockSpec((tokens, LANES), lambda j: (0, j))
    near_spec = pl.BlockSpec((2, keys, LANES), lambda j: (0, 0, j))
    near_shape = jax.ShapeDtypeStruct((2, keys, inner), jnp.bfloat16)
    return pl.pallas_call(
        grads_kernel,
        grid=(pairs,),
        in_specs=[by_pair, by_pair,
                  pl.BlockSpec((None, 8, 2 * tokens), lambda j: (j, 0, 0)),
                  near_spec, near_spec, near_spec,
                  pl.BlockSpec(bias.shape, lambda j: (0, 0))],
        out_specs=[by_pair, near_spec, near_spec, near_spec],
        out_shape=[jax.ShapeDtypeStruct((tokens, inner), jnp.bfloat16)] + [near_shape] * 3,
        cost_estimate=pl.CostEstimate(
            flops=10 * 3 * keys * tokens * inner * 2, bytes_accessed=12 * keys * inner * 2,
            transcendentals=3 * keys * tokens * 20),
        name="attention_grads",
    )(queries, grads, totals, *nearby, bias)


def local(queries, keys, values, grad_out, out_weight, windows):
    frames, row_count, col_count, inner = queries.shape
    model_width = grad_out.shape[3]
    tokens = frames * row_count * col_count
    all_frames = frames * lax.axis_size("ta")
    all_rows = row_count * lax.axis_size("ha")
    total_tokens = all_frames * all_rows * col_count
    flat_queries = queries.reshape(tokens, inner)
    flat_grad = grad_out.reshape(tokens, model_width)

    own = jnp.stack([keys.reshape(tokens, inner), values.reshape(tokens, inner)])
    below = shifted(own[:, tokens - col_count :], "ha", 1)
    above = shifted(own[:, :col_count], "ha", -1)
    chip_grad = jnp.concatenate([flat_grad, moved(flat_grad, "c", 1)], axis=0)
    wide = jnp.concatenate([below, own, above], axis=1)
    nearby = (shifted(wide, "ta", 1), wide, shifted(wide, "ta", -1))
    first, second = gathered_weight(out_weight)

    order = row_order(out_weight.shape[0])
    picks = (order[:, None] == lax.broadcasted_iota(jnp.int32, (1, inner), 1)).astype(jnp.bfloat16)
    bias = visible_keys(windows, all_frames, all_rows, row_count, col_count)

    attended, totals = attend(flat_queries, nearby, bias)
    picked = dot(attended, picks, 1, 1).astype(jnp.bfloat16)
    half = inner // 2
    chip_attended = jnp.concatenate(
        [picked[:, :half], moved(picked[:, half:], "c", 1)], axis=0
    )
    partial = (dot(chip_attended, chip_grad, 0, 0) * total_tokens ** (-0.5)).astype(jnp.bfloat16)
    weight_grad = scattered_sum(partial)

    wide_half = model_width // 2
    chip_attn = (
        dot(chip_grad[:, :wide_half], first, 1, 1) + dot(chip_grad[:, wide_half:], second, 1, 1)
    ).astype(jnp.bfloat16)
    split_attn = jnp.concatenate([chip_attn[:tokens], moved(chip_attn[tokens:], "c", 1)], axis=1)
    grad_attn = dot(split_attn, picks, 1, 0).astype(jnp.bfloat16)

    query_grad, before, here, after = attention_grads(flat_queries, grad_attn, totals, nearby, bias)
    here = (here.astype(jnp.float32) + shifted(before, "ta", -1).astype(jnp.float32)
            + shifted(after, "ta", 1).astype(jnp.float32))
    low = shifted(here[:, :col_count].astype(jnp.bfloat16), "ha", -1).astype(jnp.float32)
    high = shifted(here[:, tokens + col_count :].astype(jnp.bfloat16), "ha", 1).astype(jnp.float32)
    middle = here[:, col_count : tokens + col_count]
    rest = jnp.zeros_like(middle[:, : tokens - col_count])
    middle = (middle + jnp.concatenate([high, rest], axis=1)
              + jnp.concatenate([rest, low], axis=1)).astype(jnp.bfloat16)
    return (
        query_grad.reshape(queries.shape),
        middle[0].reshape(queries.shape),
        middle[1].reshape(queries.shape),
        weight_grad,
    )


def solution(mesh):
    tokens = P("ta", "ha", None, None)
    rows = P(("ta", "ha"), None)
    return jax.shard_map(
        local,
        mesh=mesh,
        in_specs=(tokens, tokens, tokens, tokens, rows, tokens),
        out_specs=(tokens, tokens, tokens, rows),
        check_vma=False,
    )
```

```python
import jax
import jax.numpy as jnp
from jax import lax
from jax.experimental import pallas as pl
from jax.sharding import Mesh
from jax.sharding import PartitionSpec as P

HEAD_DIM = 64
TILE_W = 8
LANES = 128
SIZES = {"x": 4, "y": 4, "z": 8, "c": 2}
AXES = {"x": ("xh", "xl"), "y": "y", "z": "z", "c": "c"}
TA = ("xh", "z")
HA = ("y", "xl", "c")
NEG = -1e30


def moved(value, dim, steps):
    n = SIZES[dim]
    return lax.ppermute(value, AXES[dim], [(i, (i + steps) % n) for i in range(n)])


def shifted(value, axis, steps):
    count = lax.axis_size(axis)
    first, last = (max(0, -steps), min(count, count - steps))
    return lax.ppermute(value, axis, [(source, source + steps) for source in range(first, last)])


def exchanged(blocks, dim):
    return lax.all_to_all(blocks, AXES[dim], 0, 0, tiled=True)


def collected(value, dim):
    return exchanged(jnp.broadcast_to(value[None], (SIZES[dim], *value.shape)), dim)


def ahead(value, dim):
    return [value] + [moved(value, dim, -k) for k in range(1, SIZES[dim])]


def exchange_sum(blocks, dim):
    return jnp.sum(exchanged(blocks, dim).astype(jnp.float32), axis=0)


def ahead_sum(pieces, dim):
    total = pieces[0].astype(jnp.float32)
    for k in range(1, SIZES[dim]):
        arrived = moved(pieces[k], dim, k)
        total = total + arrived.astype(jnp.float32)
    return total


def gathered_weight(weight):
    half = weight.shape[1] // 2
    rows = collected(weight, "z").reshape(-1, weight.shape[1])
    n = rows.shape[0]
    first = jnp.concatenate(ahead(rows[:, :half], "x"), axis=0)
    second = collected(rows[:, half:], "y")
    first = collected(first, "y").reshape(16 * n, half)
    second = jnp.stack(ahead(second, "x"), axis=1).reshape(16 * n, half)
    return first, second


def scattered_sum(partial):
    rows, width = partial.shape
    half = width // 2
    n = rows // 16
    first = partial[:, :half].reshape(4, 4 * n, half)
    second = partial[:, half:].reshape(4, 4, n, half)
    first = exchange_sum(first, "y").astype(jnp.bfloat16).reshape(4, n, half)
    second = ahead_sum([second[:, k] for k in range(4)], "x").astype(jnp.bfloat16)
    first = ahead_sum([first[k] for k in range(4)], "x").astype(jnp.bfloat16)
    second = exchange_sum(second, "y").astype(jnp.bfloat16)
    both = jnp.concatenate([first, second], axis=1).reshape(8, n // 8, width)
    return exchange_sum(both, "z")


def row_order(own_rows):
    c = lax.axis_index("c")
    shape = (2, 4, 4, 8, own_rows)
    core = (c + lax.broadcasted_iota(jnp.int32, shape, 0)) % 2
    y = lax.broadcasted_iota(jnp.int32, shape, 1)
    own_x = lax.axis_index("xh") * 2 + lax.axis_index("xl")
    x = (own_x + lax.broadcasted_iota(jnp.int32, shape, 2)) % 4
    z = lax.broadcasted_iota(jnp.int32, shape, 3)
    row = lax.broadcasted_iota(jnp.int32, shape, 4)
    number = ((x // 2) * 8 + z) * 16 + y * 4 + (x % 2) * 2 + core
    return (number * own_rows + row).reshape(-1)


def visible_keys(windows, frames_in_all, rows_in_all, row_count, col_count):
    time_index = lax.axis_index(TA)
    first_row = lax.axis_index(HA) * row_count
    extent = jnp.repeat(windows[0], TILE_W, axis=1).reshape(row_count * col_count, 3)
    shape = (3, row_count + 2, col_count, row_count, col_count)
    key_frame = lax.broadcasted_iota(jnp.int32, shape, 0) - 1
    key_row = lax.broadcasted_iota(jnp.int32, shape, 1) - 1
    key_tile = lax.broadcasted_iota(jnp.int32, shape, 2) // TILE_W
    query_row = lax.broadcasted_iota(jnp.int32, shape, 3)
    query_tile = lax.broadcasted_iota(jnp.int32, shape, 4) // TILE_W
    flat = (3 * (row_count + 2) * col_count, row_count * col_count)
    apart = [jnp.abs(key_frame), jnp.abs(key_row - query_row), jnp.abs(key_tile - query_tile)]
    inside = (
        (key_frame + time_index >= 0)
        & (key_frame + time_index < frames_in_all)
        & (key_row + first_row >= 0)
        & (key_row + first_row < rows_in_all)
    ).reshape(flat)
    for axis in range(3):
        inside = inside & (apart[axis].reshape(flat) <= extent[None, :, axis])
    return jnp.where(inside, 0.0, NEG).astype(jnp.float32)


def stacked(pair):
    lane = lax.broadcasted_iota(jnp.int32, pair.shape, 1)
    zero = jnp.zeros_like(pair)
    return jnp.concatenate(
        [jnp.where(lane < HEAD_DIM, pair, zero), jnp.where(lane < HEAD_DIM, zero, pair)], axis=0
    )


def unstacked(both):
    n = both.shape[0] // 2
    lane = lax.broadcasted_iota(jnp.int32, (n, LANES), 1)
    return jnp.where(lane < HEAD_DIM, both[:n], both[n:])


def dot(a, b, a_dim, b_dim):
    return lax.dot_general(
        a, b, (((a_dim,), (b_dim,)), ((), ())), preferred_element_type=jnp.float32
    )


def near(refs, which):
    return jnp.concatenate([ref[which] for ref in refs], axis=0)


def attend_kernel(q_ref, prev_ref, own_ref, next_ref, bias_ref, out_ref, total_ref):
    refs = (prev_ref, own_ref, next_ref)
    queries = stacked(q_ref[...] * jnp.asarray(HEAD_DIM**-0.5, jnp.bfloat16))
    scores = dot(near(refs, 0), queries, 1, 1)
    bias = bias_ref[...]
    scores = scores + jnp.concatenate([bias, bias], axis=1)
    top = jnp.max(scores, axis=0, keepdims=True)
    raised = jnp.exp(scores - top)
    total = jnp.sum(raised, axis=0, keepdims=True)
    total_ref[...] = jnp.broadcast_to(top + jnp.log(total), total_ref.shape)
    mixed = dot(near(refs, 1), raised.astype(jnp.bfloat16), 0, 0) / total
    out_ref[...] = unstacked(mixed.T).astype(jnp.bfloat16)


def grads_kernel(
    q_ref, g_ref, total_ref, prev_ref, own_ref, next_ref, bias_ref,
    dq_ref, dprev_ref, down_ref, dnext_ref,
):
    refs = (prev_ref, own_ref, next_ref)
    queries = stacked(q_ref[...] * jnp.asarray(HEAD_DIM**-0.5, jnp.bfloat16))
    grads = stacked(g_ref[...])
    keys = near(refs, 0)
    bias = bias_ref[...]
    scores = dot(keys, queries, 1, 1) + jnp.concatenate([bias, bias], axis=1)
    weights = jnp.exp(scores - total_ref[0:1, :])
    dweights = weights * dot(near(refs, 1), grads, 1, 1)
    delta = jnp.sum(dweights, axis=0, keepdims=True)
    dscores = (dweights - weights * delta).astype(jnp.bfloat16)
    dvalues = dot(weights.astype(jnp.bfloat16), grads, 1, 0)
    dkeys = dot(dscores, queries, 1, 0)
    dqueries = dot(keys, dscores, 0, 0) * HEAD_DIM**-0.5
    dq_ref[...] = unstacked(dqueries.T).astype(jnp.bfloat16)
    n = dprev_ref.shape[1]
    for i, ref in enumerate((dprev_ref, down_ref, dnext_ref)):
        ref[0] = dkeys[i * n : (i + 1) * n].astype(jnp.bfloat16)
        ref[1] = dvalues[i * n : (i + 1) * n].astype(jnp.bfloat16)


def attend(queries, nearby, bias):
    tokens, inner = queries.shape
    keys = nearby[0].shape[1]
    pairs = inner // LANES
    by_pair = pl.BlockSpec((tokens, LANES), lambda j: (0, j))
    near_spec = pl.BlockSpec((2, keys, LANES), lambda j: (0, 0, j))
    return pl.pallas_call(
        attend_kernel,
        grid=(pairs,),
        in_specs=[by_pair, near_spec, near_spec, near_spec,
                  pl.BlockSpec(bias.shape, lambda j: (0, 0))],
        out_specs=[by_pair, pl.BlockSpec((None, 8, 2 * tokens), lambda j: (j, 0, 0))],
        out_shape=[
            jax.ShapeDtypeStruct((tokens, inner), jnp.bfloat16),
            jax.ShapeDtypeStruct((pairs, 8, 2 * tokens), jnp.float32),
        ],
        cost_estimate=pl.CostEstimate(
            flops=4 * 3 * keys * tokens * inner * 2, bytes_accessed=6 * keys * inner * 2,
            transcendentals=3 * keys * tokens * 20),
        name="attend",
    )(queries, *nearby, bias)


def attention_grads(queries, grads, totals, nearby, bias):
    tokens, inner = queries.shape
    keys = nearby[0].shape[1]
    pairs = inner // LANES
    by_pair = pl.BlockSpec((tokens, LANES), lambda j: (0, j))
    near_spec = pl.BlockSpec((2, keys, LANES), lambda j: (0, 0, j))
    near_shape = jax.ShapeDtypeStruct((2, keys, inner), jnp.bfloat16)
    return pl.pallas_call(
        grads_kernel,
        grid=(pairs,),
        in_specs=[by_pair, by_pair,
                  pl.BlockSpec((None, 8, 2 * tokens), lambda j: (j, 0, 0)),
                  near_spec, near_spec, near_spec,
                  pl.BlockSpec(bias.shape, lambda j: (0, 0))],
        out_specs=[by_pair, near_spec, near_spec, near_spec],
        out_shape=[jax.ShapeDtypeStruct((tokens, inner), jnp.bfloat16)] + [near_shape] * 3,
        cost_estimate=pl.CostEstimate(
            flops=10 * 3 * keys * tokens * inner * 2, bytes_accessed=12 * keys * inner * 2,
            transcendentals=3 * keys * tokens * 20),
        name="attention_grads",
    )(queries, grads, totals, *nearby, bias)


def step(queries, keys, values, grad_out, out_weight, windows):
    frames, row_count, col_count, inner = queries.shape
    model_width = grad_out.shape[3]
    tokens = frames * row_count * col_count
    all_frames = frames * lax.axis_size(TA)
    all_rows = row_count * lax.axis_size(HA)
    total_tokens = all_frames * all_rows * col_count
    flat_queries = queries.reshape(tokens, inner)
    flat_grad = grad_out.reshape(tokens, model_width)

    own = jnp.stack([keys.reshape(tokens, inner), values.reshape(tokens, inner)])
    below = shifted(own[:, tokens - col_count :], HA, 1)
    above = shifted(own[:, :col_count], HA, -1)
    other_grad = moved(flat_grad, "c", 1)
    chip_grad = jnp.concatenate([flat_grad, other_grad], axis=0)
    wide = jnp.concatenate([below, own, above], axis=1)
    nearby = (shifted(wide, TA, 1), wide, shifted(wide, TA, -1))
    first, second = gathered_weight(out_weight)

    order = row_order(out_weight.shape[0])
    picks = (order[:, None] == lax.broadcasted_iota(jnp.int32, (1, inner), 1)).astype(jnp.bfloat16)
    bias = visible_keys(windows, all_frames, all_rows, row_count, col_count)

    attended, totals = attend(flat_queries, nearby, bias)
    picked = dot(attended, picks, 1, 1).astype(jnp.bfloat16)
    half = inner // 2
    other_attended = moved(picked[:, half:], "c", 1)
    chip_attended = jnp.concatenate([picked[:, :half], other_attended], axis=0)
    partial = (dot(chip_attended, chip_grad, 0, 0) * total_tokens ** (-0.5)).astype(jnp.bfloat16)
    weight_grad = scattered_sum(partial)

    wide_half = model_width // 2
    chip_attn = (
        dot(chip_grad[:, :wide_half], first, 1, 1) + dot(chip_grad[:, wide_half:], second, 1, 1)
    ).astype(jnp.bfloat16)
    other_attn = moved(chip_attn[tokens:], "c", 1)
    split_attn = jnp.concatenate([chip_attn[:tokens], other_attn], axis=1)
    grad_attn = dot(split_attn, picks, 1, 0).astype(jnp.bfloat16)

    query_grad, before, here, after = attention_grads(flat_queries, grad_attn, totals, nearby, bias)
    before = shifted(before, TA, -1)
    after = shifted(after, TA, 1)
    here = here.astype(jnp.float32) + before.astype(jnp.float32) + after.astype(jnp.float32)
    low = here[:, :col_count].astype(jnp.bfloat16)
    high = here[:, tokens + col_count :].astype(jnp.bfloat16)
    low = shifted(low, HA, -1)
    high = shifted(high, HA, 1)
    middle = here[:, col_count : tokens + col_count]
    rest = jnp.zeros_like(middle[:, : tokens - col_count])
    middle = (middle + jnp.concatenate([high.astype(jnp.float32), rest], axis=1)
              + jnp.concatenate([rest, low.astype(jnp.float32)], axis=1)).astype(jnp.bfloat16)
    return (
        query_grad.reshape(queries.shape),
        middle[0].reshape(queries.shape),
        middle[1].reshape(queries.shape),
        weight_grad,
    )


def solution(mesh):
    fine = Mesh(mesh.devices.reshape(2, 8, 4, 2, 2), ("xh", "z", "y", "xl", "c"))
    tokens = P(TA, HA, None, None)
    rows = P(TA + HA, None)
    return jax.shard_map(
        step,
        mesh=fine,
        in_specs=(tokens, tokens, tokens, tokens, rows, tokens),
        out_specs=(tokens, tokens, tokens, rows),
        check_vma=False,
    )
```

```python
import jax
import jax.numpy as jnp
from jax import lax
from jax.experimental import pallas as pl
from jax.sharding import Mesh
from jax.sharding import PartitionSpec as P

HEAD_DIM = 64
TILE_W = 8
LANES = 128
NEG = -1e30

MESH_SHAPE = (2, 8, 4, 2, 2)
MESH_NAMES = ("xh", "z", "y", "xl", "c")
TA = ("xh", "z")
HA = ("y", "xl", "c")
XY = ("xh", "xl", "y")
PER_STEP = 5


def shifted(value, axis, steps):
    count = lax.axis_size(axis)
    first, last = (max(0, -steps), min(count, count - steps))
    return lax.ppermute(value, axis, [(source, source + steps) for source in range(first, last)])


def exchanged(blocks, axis):
    return lax.all_to_all(blocks, axis, 0, 0, tiled=True)


def flipped(value, flip_y, flip_core):
    pairs = []
    for y in range(4):
        for c in range(2):
            pairs.append((y * 2 + c, (y ^ flip_y) * 2 + (c ^ flip_core)))
    return lax.ppermute(value, ("y", "c"), pairs)


def gathered_weight(weight):
    width = weight.shape[1]
    rows = exchanged(jnp.broadcast_to(weight[None], (8, *weight.shape)), "z")
    rows = rows.reshape(-1, width)
    halves = jnp.swapaxes(rows.reshape(-1, 2, width // 2), 0, 1)
    blocks = jnp.broadcast_to(halves[None], (8, *halves.shape))
    blocks = blocks.reshape(16, *halves.shape[1:])
    return exchanged(blocks, XY).reshape(-1, width // 2)


def scattered_sum(partial):
    rows, half = partial.shape
    n = rows // 16
    blocks = exchanged(partial.reshape(16, n, half), XY)
    halves = jnp.sum(blocks.reshape(8, 2, n, half).astype(jnp.float32), axis=0)
    both = jnp.concatenate([halves[0], halves[1]], axis=1).astype(jnp.bfloat16)
    blocks = exchanged(both.reshape(8, n // 8, 2 * half), "z")
    return jnp.sum(blocks.astype(jnp.float32), axis=0)


def row_order(own_rows):
    c = lax.axis_index("c")
    shape = (2, 4, 4, 8, own_rows)
    core = (c + lax.broadcasted_iota(jnp.int32, shape, 0)) % 2
    x = lax.broadcasted_iota(jnp.int32, shape, 1)
    y = lax.broadcasted_iota(jnp.int32, shape, 2)
    z = lax.broadcasted_iota(jnp.int32, shape, 3)
    row = lax.broadcasted_iota(jnp.int32, shape, 4)
    number = ((x // 2) * 8 + z) * 16 + y * 4 + (x % 2) * 2 + core
    return (number * own_rows + row).reshape(-1)


def key_places(row_count, col_count):
    centre = (3, row_count, col_count)
    edges = (2, 3, col_count)

    def joined(first, second):
        return jnp.concatenate([first.reshape(-1), second.reshape(-1)])

    iota = lax.broadcasted_iota
    frame = joined(iota(jnp.int32, centre, 0), iota(jnp.int32, edges, 1)) - 1
    edge_row = iota(jnp.int32, edges, 0) * (row_count + 1) - 1
    row = joined(iota(jnp.int32, centre, 1), edge_row)
    tile = joined(iota(jnp.int32, centre, 2), iota(jnp.int32, edges, 2)) // TILE_W
    return frame, row, tile


def visible_keys(windows, frames_in_all, rows_in_all, row_count, col_count):
    time_index = lax.axis_index(TA)
    first_row = lax.axis_index(HA) * row_count
    tokens = row_count * col_count
    extent = jnp.repeat(windows[0], TILE_W, axis=1).reshape(tokens, 3)
    frame, row, tile = key_places(row_count, col_count)
    query = lax.broadcasted_iota(jnp.int32, (1, tokens), 1)
    inside = (
        (frame + time_index >= 0)
        & (frame + time_index < frames_in_all)
        & (row + first_row >= 0)
        & (row + first_row < rows_in_all)
    )[:, None]
    query_row = query // col_count
    query_tile = query % col_count // TILE_W
    inside = inside & (jnp.abs(frame)[:, None] <= extent[None, :, 0])
    inside = inside & (jnp.abs(row[:, None] - query_row) <= extent[None, :, 1])
    inside = inside & (jnp.abs(tile[:, None] - query_tile) <= extent[None, :, 2])
    return jnp.where(inside, 0.0, NEG).astype(jnp.float32)


def stacked(pair):
    lane = lax.broadcasted_iota(jnp.int32, pair.shape, 1)
    zero = jnp.zeros_like(pair)
    return jnp.concatenate(
        [jnp.where(lane < HEAD_DIM, pair, zero), jnp.where(lane < HEAD_DIM, zero, pair)], axis=0
    )


def unstacked(both):
    n = both.shape[0] // 2
    lane = lax.broadcasted_iota(jnp.int32, (n, LANES), 1)
    return jnp.where(lane < HEAD_DIM, both[:n], both[n:])


def dot(a, b, a_dim, b_dim):
    return lax.dot_general(
        a, b, (((a_dim,), (b_dim,)), ((), ())), preferred_element_type=jnp.float32
    )


def near(refs, which, lanes):
    return jnp.concatenate([ref[which, :, lanes] for ref in refs], axis=0)


def scaled_queries(q_ref, lanes):
    return stacked(q_ref[:, lanes] * jnp.asarray(HEAD_DIM**-0.5, jnp.bfloat16))


def attend_kernel(q_ref, *refs):
    near_refs = refs[:5]
    bias_ref, out_ref, total_ref = refs[5:]
    for i in range(PER_STEP):
        lanes = slice(i * LANES, (i + 1) * LANES)
        queries = scaled_queries(q_ref, lanes)
        scores = dot(near(near_refs, 0, lanes), queries, 1, 1)
        bias = bias_ref[...]
        scores = scores + jnp.concatenate([bias, bias], axis=1)
        top = jnp.max(scores, axis=0, keepdims=True)
        raised = jnp.exp(scores - top)
        total = jnp.sum(raised, axis=0, keepdims=True)
        total_ref[i] = jnp.broadcast_to(top + jnp.log(total), total_ref.shape[1:])
        mixed = dot(near(near_refs, 1, lanes), raised.astype(jnp.bfloat16), 0, 0) / total
        out_ref[:, lanes] = unstacked(mixed.T).astype(jnp.bfloat16)


def grads_kernel(q_ref, g_ref, total_ref, *refs):
    near_refs = refs[:5]
    bias_ref, dq_ref = refs[5:7]
    out_refs = refs[7:]
    for i in range(PER_STEP):
        lanes = slice(i * LANES, (i + 1) * LANES)
        queries = scaled_queries(q_ref, lanes)
        grads = stacked(g_ref[:, lanes])
        keys = near(near_refs, 0, lanes)
        bias = bias_ref[...]
        scores = dot(keys, queries, 1, 1) + jnp.concatenate([bias, bias], axis=1)
        weights = jnp.exp(scores - total_ref[i, 0:1, :])
        dweights = weights * dot(near(near_refs, 1, lanes), grads, 1, 1)
        delta = jnp.sum(dweights, axis=0, keepdims=True)
        dscores = (dweights - weights * delta).astype(jnp.bfloat16)
        dvalues = dot(weights.astype(jnp.bfloat16), grads, 1, 0)
        dkeys = dot(dscores, queries, 1, 0)
        dqueries = dot(keys, dscores, 0, 0) * HEAD_DIM**-0.5
        dq_ref[:, lanes] = unstacked(dqueries.T).astype(jnp.bfloat16)
        first = 0
        for ref in out_refs:
            last = first + ref.shape[1]
            ref[0, :, lanes] = dkeys[first:last].astype(jnp.bfloat16)
            ref[1, :, lanes] = dvalues[first:last].astype(jnp.bfloat16)
            first = last


def specs(tokens, nearby, bias):
    width = PER_STEP * LANES
    by_pair = pl.BlockSpec((tokens, width), lambda j: (0, j))
    near_specs = [pl.BlockSpec((*x.shape[:2], width), lambda j: (0, 0, j)) for x in nearby]
    totals = pl.BlockSpec((PER_STEP, 8, 2 * tokens), lambda j: (j, 0, 0))
    return by_pair, near_specs, totals, pl.BlockSpec(bias.shape, lambda j: (0, 0))


def attend(queries, nearby, bias):
    tokens, inner = queries.shape
    keys = bias.shape[0]
    by_pair, near_specs, totals, bias_spec = specs(tokens, nearby, bias)
    return pl.pallas_call(
        attend_kernel,
        grid=(inner // LANES // PER_STEP,),
        in_specs=[by_pair, *near_specs, bias_spec],
        out_specs=[by_pair, totals],
        out_shape=[
            jax.ShapeDtypeStruct((tokens, inner), jnp.bfloat16),
            jax.ShapeDtypeStruct((inner // LANES, 8, 2 * tokens), jnp.float32),
        ],
        cost_estimate=pl.CostEstimate(
            flops=8 * keys * tokens * inner, bytes_accessed=4 * keys * inner,
            transcendentals=keys * tokens * 20),
        name="attend",
    )(queries, *nearby, bias)


def attention_grads(queries, grads, totals, nearby, bias):
    tokens, inner = queries.shape
    keys = bias.shape[0]
    by_pair, near_specs, totals_spec, bias_spec = specs(tokens, nearby, bias)
    return pl.pallas_call(
        grads_kernel,
        grid=(inner // LANES // PER_STEP,),
        in_specs=[by_pair, by_pair, totals_spec, *near_specs, bias_spec],
        out_specs=[by_pair, *near_specs],
        out_shape=[jax.ShapeDtypeStruct((tokens, inner), jnp.bfloat16)]
        + [jax.ShapeDtypeStruct(x.shape, jnp.bfloat16) for x in nearby],
        cost_estimate=pl.CostEstimate(
            flops=20 * keys * tokens * inner, bytes_accessed=8 * keys * inner,
            transcendentals=keys * tokens * 20),
        name="attention_grads",
    )(queries, grads, totals, *nearby, bias)


def step(queries, keys, values, grad_out, out_weight, windows):
    frames, row_count, col_count, inner = queries.shape
    model_width = grad_out.shape[3]
    tokens = frames * row_count * col_count
    all_frames = frames * lax.axis_size(TA)
    all_rows = row_count * lax.axis_size(HA)
    total_tokens = all_frames * all_rows * col_count
    flat_queries = queries.reshape(tokens, inner)
    flat_grad = grad_out.reshape(tokens, model_width)

    own = jnp.stack([keys.reshape(tokens, inner), values.reshape(tokens, inner)])
    centre = (shifted(own, TA, 1), own, shifted(own, TA, -1))
    top = jnp.concatenate([x[:, :col_count] for x in centre], axis=1)
    bottom = jnp.concatenate([x[:, tokens - col_count :] for x in centre], axis=1)
    nearby = (*centre, shifted(bottom, HA, 1), shifted(top, HA, -1))

    wide_half = model_width // 2
    odd = lax.axis_index("y") % 2
    from_pair = flipped(
        lax.dynamic_slice_in_dim(flat_grad, (1 - odd) * wide_half, wide_half, axis=1), 1, 0
    )
    mine = lax.dynamic_slice_in_dim(flat_grad, odd * wide_half, wide_half, axis=1)
    mine = jnp.stack([mine, from_pair])
    others = flipped(mine, 0, 1)
    group_grad = jnp.stack([mine, others], axis=1).reshape(4 * tokens, wide_half)

    weight = gathered_weight(out_weight)
    order = row_order(out_weight.shape[0])
    picks = (order[:, None] == lax.broadcasted_iota(jnp.int32, (1, inner), 1)).astype(jnp.bfloat16)
    bias = visible_keys(windows, all_frames, all_rows, row_count, col_count)

    attended, totals = attend(flat_queries, nearby, bias)
    picked = dot(attended, picks, 1, 1).astype(jnp.bfloat16)
    half = inner // 2
    group_attended = jnp.concatenate(
        [picked[:, :half], flipped(picked[:, half:], 0, 1),
         flipped(picked[:, :half], 1, 0), flipped(picked[:, half:], 1, 1)], axis=0
    )
    partial = dot(group_attended, group_grad, 0, 0) * total_tokens ** (-0.5)
    partial = partial.astype(jnp.bfloat16)
    weight_grad = scattered_sum(partial)

    group_attn = dot(group_grad, weight, 1, 1)
    sent = group_attn.astype(jnp.bfloat16)
    here_other = flipped(sent[tokens : 2 * tokens], 0, 1)
    pair_own = flipped(sent[2 * tokens : 3 * tokens], 1, 0)
    pair_other = flipped(sent[3 * tokens :], 1, 1)
    own_half = group_attn[:tokens] + pair_own.astype(jnp.float32)
    other_half = here_other.astype(jnp.float32) + pair_other.astype(jnp.float32)
    split_attn = jnp.concatenate([own_half, other_half], axis=1).astype(jnp.bfloat16)
    grad_attn = dot(split_attn, picks, 1, 0).astype(jnp.bfloat16)

    query_grad, *pieces = attention_grads(flat_queries, grad_attn, totals, nearby, bias)
    to_bottom = shifted(pieces[3], HA, -1).astype(jnp.float32)
    to_top = shifted(pieces[4], HA, 1).astype(jnp.float32)
    rest = jnp.zeros_like(pieces[0][:, : tokens - col_count], jnp.float32)

    def with_edges(i):
        at = slice(i * col_count, (i + 1) * col_count)
        return (pieces[i].astype(jnp.float32)
                + jnp.concatenate([to_top[:, at], rest], axis=1)
                + jnp.concatenate([rest, to_bottom[:, at]], axis=1))

    before, here, after = [with_edges(i) for i in range(3)]
    before = shifted(before.astype(jnp.bfloat16), TA, -1)
    after = shifted(after.astype(jnp.bfloat16), TA, 1)
    total = (here + before.astype(jnp.float32) + after.astype(jnp.float32)).astype(jnp.bfloat16)
    return (
        query_grad.reshape(queries.shape),
        total[0].reshape(queries.shape),
        total[1].reshape(queries.shape),
        weight_grad,
    )


def solution(mesh):
    fine = Mesh(mesh.devices.reshape(MESH_SHAPE), MESH_NAMES)
    tokens = P(TA, HA, None, None)
    rows = P(TA + HA, None)
    return jax.shard_map(
        step,
        mesh=fine,
        in_specs=(tokens, tokens, tokens, tokens, rows, tokens),
        out_specs=(tokens, tokens, tokens, rows),
        check_vma=False,
    )
```

```python
import jax
import jax.numpy as jnp
from jax import lax
from jax.experimental import pallas as pl
from jax.sharding import Mesh
from jax.sharding import PartitionSpec as P

HEAD_DIM = 64
TILE_W = 8
LANES = 128
NEG = -1e30

MESH_SHAPE = (2, 8, 4, 2, 2)
MESH_NAMES = ("xh", "z", "y", "xl", "c")
TA = ("xh", "z")
HA = ("y", "xl", "c")
XY = ("xh", "xl", "y")
PER_STEP = 5


def shifted(value, axis, steps):
    count = lax.axis_size(axis)
    first, last = (max(0, -steps), min(count, count - steps))
    return lax.ppermute(value, axis, [(source, source + steps) for source in range(first, last)])


def exchanged(blocks, axis):
    return lax.all_to_all(blocks, axis, 0, 0, tiled=True)


def flipped(value, flip_y, flip_core):
    pairs = []
    for y in range(4):
        for c in range(2):
            pairs.append((y * 2 + c, (y ^ flip_y) * 2 + (c ^ flip_core)))
    return lax.ppermute(value, ("y", "c"), pairs)


def gathered_weight(weight):
    width = weight.shape[1]
    rows = exchanged(jnp.broadcast_to(weight[None], (8, *weight.shape)), "z")
    rows = rows.reshape(-1, width)
    halves = jnp.swapaxes(rows.reshape(-1, 2, width // 2), 0, 1)
    blocks = jnp.broadcast_to(halves[None], (8, *halves.shape))
    blocks = blocks.reshape(16, *halves.shape[1:])
    return exchanged(blocks, XY).reshape(-1, width // 2)


def scattered_sum(partial):
    rows, half = partial.shape
    n = rows // 16
    blocks = exchanged(partial.reshape(16, n, half), XY)
    halves = jnp.sum(blocks.reshape(8, 2, n, half).astype(jnp.float32), axis=0)
    both = jnp.concatenate([halves[0], halves[1]], axis=1).astype(jnp.bfloat16)
    blocks = exchanged(both.reshape(8, n // 8, 2 * half), "z")
    return jnp.sum(blocks.astype(jnp.float32), axis=0)


def row_order(own_rows):
    c = lax.axis_index("c")
    shape = (2, 4, 4, 8, own_rows)
    core = (c + lax.broadcasted_iota(jnp.int32, shape, 0)) % 2
    x = lax.broadcasted_iota(jnp.int32, shape, 1)
    y = lax.broadcasted_iota(jnp.int32, shape, 2)
    z = lax.broadcasted_iota(jnp.int32, shape, 3)
    row = lax.broadcasted_iota(jnp.int32, shape, 4)
    number = ((x // 2) * 8 + z) * 16 + y * 4 + (x % 2) * 2 + core
    return (number * own_rows + row).reshape(-1)


def visible_groups(windows, frames_in_all, rows_in_all, row_count, col_count):
    time_index = lax.axis_index(TA)
    first_row = lax.axis_index(HA) * row_count
    tokens = row_count * col_count
    extent = jnp.repeat(windows[0], TILE_W, axis=1).reshape(tokens, 3)
    tiles = col_count // TILE_W
    group = lax.broadcasted_iota(jnp.int32, (tokens, LANES), 1)
    query = lax.broadcasted_iota(jnp.int32, (tokens, LANES), 0)
    frame = group // ((row_count + 2) * tiles) - 1
    row = group // tiles % (row_count + 2) - 1
    tile = group % tiles
    inside = (
        (frame + time_index >= 0)
        & (frame + time_index < frames_in_all)
        & (row + first_row >= 0)
        & (row + first_row < rows_in_all)
        & (jnp.abs(frame) <= extent[:, 0:1])
        & (jnp.abs(row - query // col_count) <= extent[:, 1:2])
        & (jnp.abs(tile - query % col_count // TILE_W) <= extent[:, 2:3])
    )
    return jnp.where(inside, 0.0, NEG).astype(jnp.bfloat16)


def key_groups(row_count, col_count):
    keys = 3 * (row_count + 2) * col_count
    key = lax.broadcasted_iota(jnp.int32, (keys, LANES), 0)
    group = lax.broadcasted_iota(jnp.int32, (keys, LANES), 1)
    return (key // TILE_W == group).astype(jnp.bfloat16)


def stacked(pair):
    lane = lax.broadcasted_iota(jnp.int32, pair.shape, 1)
    zero = jnp.zeros_like(pair)
    return jnp.concatenate(
        [jnp.where(lane < HEAD_DIM, pair, zero), jnp.where(lane < HEAD_DIM, zero, pair)], axis=0
    )


def unstacked(both):
    n = both.shape[0] // 2
    lane = lax.broadcasted_iota(jnp.int32, (n, LANES), 1)
    return jnp.where(lane < HEAD_DIM, both[:n], both[n:])


def dot(a, b, a_dim, b_dim):
    return lax.dot_general(
        a, b, (((a_dim,), (b_dim,)), ((), ())), preferred_element_type=jnp.float32
    )


def near(refs, which, lanes):
    return jnp.concatenate([ref[which, :, lanes] for ref in refs], axis=0)


def scaled_queries(q_ref, lanes):
    return stacked(q_ref[:, lanes] * jnp.asarray(HEAD_DIM**-0.5, jnp.bfloat16))


def masked_scores(keys, groups_ref, queries, seen_ref):
    seen = seen_ref[...]
    wide_keys = jnp.concatenate([keys, groups_ref[...]], axis=1)
    wide_queries = jnp.concatenate([queries, jnp.concatenate([seen, seen], axis=0)], axis=1)
    return dot(wide_keys, wide_queries, 1, 1)


def attend_kernel(q_ref, *refs):
    near_refs = refs[:3]
    groups_ref, seen_ref, out_ref, total_ref = refs[3:]
    for i in range(PER_STEP):
        lanes = slice(i * LANES, (i + 1) * LANES)
        queries = scaled_queries(q_ref, lanes)
        scores = masked_scores(near(near_refs, 0, lanes), groups_ref, queries, seen_ref)
        top = jnp.max(scores, axis=0, keepdims=True)
        raised = jnp.exp(scores - top)
        total = jnp.sum(raised, axis=0, keepdims=True)
        total_ref[i] = jnp.broadcast_to(top + jnp.log(total), total_ref.shape[1:])
        mixed = dot(near(near_refs, 1, lanes), raised.astype(jnp.bfloat16), 0, 0) / total
        out_ref[:, lanes] = unstacked(mixed.T).astype(jnp.bfloat16)


def grads_kernel(q_ref, g_ref, total_ref, *refs):
    near_refs = refs[:3]
    groups_ref, seen_ref, dq_ref = refs[3:6]
    out_refs = refs[6:]
    for i in range(PER_STEP):
        lanes = slice(i * LANES, (i + 1) * LANES)
        queries = scaled_queries(q_ref, lanes)
        grads = stacked(g_ref[:, lanes])
        keys = near(near_refs, 0, lanes)
        scores = masked_scores(keys, groups_ref, queries, seen_ref)
        weights = jnp.exp(scores - total_ref[i, 0:1, :])
        dweights = weights * dot(near(near_refs, 1, lanes), grads, 1, 1)
        delta = jnp.sum(dweights, axis=0, keepdims=True)
        dscores = (dweights - weights * delta).astype(jnp.bfloat16)
        dvalues = dot(weights.astype(jnp.bfloat16), grads, 1, 0)
        dkeys = dot(dscores, queries, 1, 0)
        dqueries = dot(keys, dscores, 0, 0) * HEAD_DIM**-0.5
        dq_ref[:, lanes] = unstacked(dqueries.T).astype(jnp.bfloat16)
        first = 0
        for ref in out_refs:
            last = first + ref.shape[1]
            ref[0, :, lanes] = dkeys[first:last].astype(jnp.bfloat16)
            ref[1, :, lanes] = dvalues[first:last].astype(jnp.bfloat16)
            first = last


def specs(tokens, nearby, mask):
    width = PER_STEP * LANES
    by_pair = pl.BlockSpec((tokens, width), lambda j: (0, j))
    near_specs = [pl.BlockSpec((*x.shape[:2], width), lambda j: (0, 0, j)) for x in nearby]
    totals = pl.BlockSpec((PER_STEP, 8, 2 * tokens), lambda j: (j, 0, 0))
    return by_pair, near_specs, totals, [pl.BlockSpec(x.shape, lambda j: (0, 0)) for x in mask]


def attend(queries, nearby, mask):
    tokens, inner = queries.shape
    keys = mask[0].shape[0]
    by_pair, near_specs, totals, mask_specs = specs(tokens, nearby, mask)
    return pl.pallas_call(
        attend_kernel,
        grid=(inner // LANES // PER_STEP,),
        in_specs=[by_pair, *near_specs, *mask_specs],
        out_specs=[by_pair, totals],
        out_shape=[
            jax.ShapeDtypeStruct((tokens, inner), jnp.bfloat16),
            jax.ShapeDtypeStruct((inner // LANES, 8, 2 * tokens), jnp.float32),
        ],
        cost_estimate=pl.CostEstimate(
            flops=8 * keys * tokens * inner, bytes_accessed=4 * keys * inner,
            transcendentals=keys * tokens * 20),
        name="attend",
    )(queries, *nearby, *mask)


def attention_grads(queries, grads, totals, nearby, mask):
    tokens, inner = queries.shape
    keys = mask[0].shape[0]
    by_pair, near_specs, totals_spec, mask_specs = specs(tokens, nearby, mask)
    return pl.pallas_call(
        grads_kernel,
        grid=(inner // LANES // PER_STEP,),
        in_specs=[by_pair, by_pair, totals_spec, *near_specs, *mask_specs],
        out_specs=[by_pair, *near_specs],
        out_shape=[jax.ShapeDtypeStruct((tokens, inner), jnp.bfloat16)]
        + [jax.ShapeDtypeStruct(x.shape, jnp.bfloat16) for x in nearby],
        cost_estimate=pl.CostEstimate(
            flops=20 * keys * tokens * inner, bytes_accessed=8 * keys * inner,
            transcendentals=keys * tokens * 20),
        name="attention_grads",
    )(queries, grads, totals, *nearby, *mask)


def step(queries, keys, values, grad_out, out_weight, windows):
    frames, row_count, col_count, inner = queries.shape
    model_width = grad_out.shape[3]
    tokens = frames * row_count * col_count
    all_frames = frames * lax.axis_size(TA)
    all_rows = row_count * lax.axis_size(HA)
    total_tokens = all_frames * all_rows * col_count
    flat_queries = queries.reshape(tokens, inner)
    flat_grad = grad_out.reshape(tokens, model_width)

    own = jnp.stack([keys.reshape(tokens, inner), values.reshape(tokens, inner)])
    below = shifted(own[:, tokens - col_count :], HA, 1)
    above = shifted(own[:, :col_count], HA, -1)
    wide = jnp.concatenate([below, own, above], axis=1)
    nearby = (shifted(wide, TA, 1), wide, shifted(wide, TA, -1))

    wide_half = model_width // 2
    odd = lax.axis_index("y") % 2
    from_pair = flipped(
        lax.dynamic_slice_in_dim(flat_grad, (1 - odd) * wide_half, wide_half, axis=1), 1, 0
    )
    mine = lax.dynamic_slice_in_dim(flat_grad, odd * wide_half, wide_half, axis=1)
    mine = jnp.stack([mine, from_pair])
    others = flipped(mine, 0, 1)
    group_grad = jnp.stack([mine, others], axis=1).reshape(4 * tokens, wide_half)

    weight = gathered_weight(out_weight)
    order = row_order(out_weight.shape[0])
    picks = (order[:, None] == lax.broadcasted_iota(jnp.int32, (1, inner), 1)).astype(jnp.bfloat16)
    mask = (
        key_groups(row_count, col_count),
        visible_groups(windows, all_frames, all_rows, row_count, col_count),
    )

    attended, totals = attend(flat_queries, nearby, mask)
    picked = dot(attended, picks, 1, 1).astype(jnp.bfloat16)
    half = inner // 2
    group_attended = jnp.concatenate(
        [picked[:, :half], flipped(picked[:, half:], 0, 1),
         flipped(picked[:, :half], 1, 0), flipped(picked[:, half:], 1, 1)], axis=0
    )
    partial = dot(group_attended, group_grad, 0, 0) * total_tokens ** (-0.5)
    partial = partial.astype(jnp.bfloat16)
    weight_grad = scattered_sum(partial)

    group_attn = dot(group_grad, weight, 1, 1)
    sent = group_attn.astype(jnp.bfloat16)
    here_other = flipped(sent[tokens : 2 * tokens], 0, 1)
    pair_own = flipped(sent[2 * tokens : 3 * tokens], 1, 0)
    pair_other = flipped(sent[3 * tokens :], 1, 1)
    own_half = group_attn[:tokens] + pair_own.astype(jnp.float32)
    other_half = here_other.astype(jnp.float32) + pair_other.astype(jnp.float32)
    split_attn = jnp.concatenate([own_half, other_half], axis=1).astype(jnp.bfloat16)
    grad_attn = dot(split_attn, picks, 1, 0).astype(jnp.bfloat16)

    query_grad, before, here, after = attention_grads(flat_queries, grad_attn, totals, nearby, mask)
    before = shifted(before, TA, -1)
    after = shifted(after, TA, 1)
    here = here.astype(jnp.float32) + before.astype(jnp.float32) + after.astype(jnp.float32)
    low = here[:, :col_count].astype(jnp.bfloat16)
    high = here[:, tokens + col_count :].astype(jnp.bfloat16)
    low = shifted(low, HA, -1).astype(jnp.float32)
    high = shifted(high, HA, 1).astype(jnp.float32)
    rest = jnp.zeros_like(here[:, : tokens - col_count])
    total = (here[:, col_count : tokens + col_count] + jnp.concatenate([high, rest], axis=1)
             + jnp.concatenate([rest, low], axis=1)).astype(jnp.bfloat16)
    return (
        query_grad.reshape(queries.shape),
        total[0].reshape(queries.shape),
        total[1].reshape(queries.shape),
        weight_grad,
    )


def solution(mesh):
    fine = Mesh(mesh.devices.reshape(MESH_SHAPE), MESH_NAMES)
    tokens = P(TA, HA, None, None)
    rows = P(TA + HA, None)
    return jax.shard_map(
        step,
        mesh=fine,
        in_specs=(tokens, tokens, tokens, tokens, rows, tokens),
        out_specs=(tokens, tokens, tokens, rows),
        check_vma=False,
    )
```

```python
import jax
import jax.numpy as jnp
from jax import lax
from jax.experimental import pallas as pl
from jax.sharding import Mesh
from jax.sharding import PartitionSpec as P

HEAD_DIM = 64
TILE_W = 8
LANES = 128
NEG = -1e30

MESH_SHAPE = (2, 8, 4, 2, 2)
MESH_NAMES = ("xh", "z", "y", "xl", "c")
TA = ("xh", "z")
HA = ("y", "xl", "c")
XY = ("xh", "xl", "y")
PER_STEP = 5


def shifted(value, axis, steps):
    count = lax.axis_size(axis)
    first, last = (max(0, -steps), min(count, count - steps))
    return lax.ppermute(value, axis, [(source, source + steps) for source in range(first, last)])


def exchanged(blocks, axis):
    return lax.all_to_all(blocks, axis, 0, 0, tiled=True)


def flipped(value, flip_y, flip_core):
    pairs = []
    for y in range(4):
        for c in range(2):
            pairs.append((y * 2 + c, (y ^ flip_y) * 2 + (c ^ flip_core)))
    return lax.ppermute(value, ("y", "c"), pairs)


def gathered_weight(weight):
    width = weight.shape[1]
    rows = exchanged(jnp.broadcast_to(weight[None], (8, *weight.shape)), "z")
    rows = rows.reshape(-1, width)
    halves = jnp.swapaxes(rows.reshape(-1, 2, width // 2), 0, 1)
    blocks = jnp.broadcast_to(halves[None], (8, *halves.shape))
    blocks = blocks.reshape(16, *halves.shape[1:])
    return exchanged(blocks, XY).reshape(-1, width // 2)


def scattered_sum(partial):
    rows, half = partial.shape
    n = rows // 16
    blocks = exchanged(partial.reshape(16, n, half), XY)
    halves = jnp.sum(blocks.reshape(8, 2, n, half).astype(jnp.float32), axis=0)
    both = jnp.concatenate([halves[0], halves[1]], axis=1).astype(jnp.bfloat16)
    blocks = exchanged(both.reshape(8, n // 8, 2 * half), "z")
    return jnp.sum(blocks.astype(jnp.float32), axis=0)


def row_order(own_rows):
    c = lax.axis_index("c")
    shape = (2, 4, 4, 8, own_rows)
    core = (c + lax.broadcasted_iota(jnp.int32, shape, 0)) % 2
    x = lax.broadcasted_iota(jnp.int32, shape, 1)
    y = lax.broadcasted_iota(jnp.int32, shape, 2)
    z = lax.broadcasted_iota(jnp.int32, shape, 3)
    row = lax.broadcasted_iota(jnp.int32, shape, 4)
    number = ((x // 2) * 8 + z) * 16 + y * 4 + (x % 2) * 2 + core
    return (number * own_rows + row).reshape(-1)


def visible_groups(windows, frames_in_all, rows_in_all, row_count, col_count):
    time_index = lax.axis_index(TA)
    first_row = lax.axis_index(HA) * row_count
    tokens = row_count * col_count
    extent = jnp.repeat(windows[0], TILE_W, axis=1).reshape(tokens, 3)
    tiles = col_count // TILE_W
    group = lax.broadcasted_iota(jnp.int32, (tokens, LANES), 1)
    query = lax.broadcasted_iota(jnp.int32, (tokens, LANES), 0)
    frame = group // ((row_count + 2) * tiles) - 1
    row = group // tiles % (row_count + 2) - 1
    tile = group % tiles
    inside = (
        (frame + time_index >= 0)
        & (frame + time_index < frames_in_all)
        & (row + first_row >= 0)
        & (row + first_row < rows_in_all)
        & (jnp.abs(frame) <= extent[:, 0:1])
        & (jnp.abs(row - query // col_count) <= extent[:, 1:2])
        & (jnp.abs(tile - query % col_count // TILE_W) <= extent[:, 2:3])
    )
    return jnp.where(inside, 0.0, NEG).astype(jnp.bfloat16)


def key_groups(row_count, col_count):
    keys = 3 * (row_count + 2) * col_count
    key = lax.broadcasted_iota(jnp.int32, (keys, LANES), 0)
    group = lax.broadcasted_iota(jnp.int32, (keys, LANES), 1)
    return (key // TILE_W == group).astype(jnp.bfloat16)


def stacked(pair):
    lane = lax.broadcasted_iota(jnp.int32, pair.shape, 1)
    zero = jnp.zeros_like(pair)
    return jnp.concatenate(
        [jnp.where(lane < HEAD_DIM, pair, zero), jnp.where(lane < HEAD_DIM, zero, pair)], axis=0
    )


def unstacked(both):
    n = both.shape[0] // 2
    lane = lax.broadcasted_iota(jnp.int32, (n, LANES), 1)
    return jnp.where(lane < HEAD_DIM, both[:n], both[n:])


def dot(a, b, a_dim, b_dim):
    return lax.dot_general(
        a, b, (((a_dim,), (b_dim,)), ((), ())), preferred_element_type=jnp.float32
    )


def near(refs, which, lanes):
    return jnp.concatenate([ref[which, :, lanes] for ref in refs], axis=0)


def scaled_queries(q_ref, lanes):
    return stacked(q_ref[:, lanes] * jnp.asarray(HEAD_DIM**-0.5, jnp.bfloat16))


def masked_scores(keys, groups_ref, queries, seen_ref):
    seen = seen_ref[...]
    wide_keys = jnp.concatenate([keys, groups_ref[...]], axis=1)
    wide_queries = jnp.concatenate([queries, jnp.concatenate([seen, seen], axis=0)], axis=1)
    return dot(wide_keys, wide_queries, 1, 1)


def attend_kernel(q_ref, *refs):
    near_refs = refs[:3]
    groups_ref, seen_ref, out_ref, total_ref = refs[3:]
    for i in range(PER_STEP):
        lanes = slice(i * LANES, (i + 1) * LANES)
        queries = scaled_queries(q_ref, lanes)
        scores = masked_scores(near(near_refs, 0, lanes), groups_ref, queries, seen_ref)
        top = jnp.max(scores, axis=0, keepdims=True)
        raised = jnp.exp(scores - top)
        total = jnp.sum(raised, axis=0, keepdims=True)
        total_ref[i] = jnp.broadcast_to(top + jnp.log(total), total_ref.shape[1:])
        mixed = dot(near(near_refs, 1, lanes), raised.astype(jnp.bfloat16), 0, 0) / total
        out_ref[:, lanes] = unstacked(mixed.T).astype(jnp.bfloat16)


def grads_kernel(q_ref, g_ref, total_ref, *refs):
    near_refs = refs[:3]
    groups_ref, seen_ref, dq_ref = refs[3:6]
    out_refs = refs[6:]
    for i in range(PER_STEP):
        lanes = slice(i * LANES, (i + 1) * LANES)
        queries = scaled_queries(q_ref, lanes)
        grads = stacked(g_ref[:, lanes])
        keys = near(near_refs, 0, lanes)
        scores = masked_scores(keys, groups_ref, queries, seen_ref)
        weights = jnp.exp(scores - total_ref[i, 0:1, :])
        dweights = weights * dot(near(near_refs, 1, lanes), grads, 1, 1)
        delta = jnp.sum(dweights, axis=0, keepdims=True)
        dscores = (dweights - weights * delta).astype(jnp.bfloat16)
        dvalues = dot(weights.astype(jnp.bfloat16), grads, 1, 0)
        dkeys = dot(dscores, queries, 1, 0)
        dqueries = dot(keys, dscores, 0, 0) * HEAD_DIM**-0.5
        dq_ref[:, lanes] = unstacked(dqueries.T).astype(jnp.bfloat16)
        first = 0
        for ref in out_refs:
            last = first + ref.shape[1]
            ref[0, :, lanes] = dkeys[first:last].astype(jnp.bfloat16)
            ref[1, :, lanes] = dvalues[first:last].astype(jnp.bfloat16)
            first = last


def specs(tokens, nearby, mask):
    width = PER_STEP * LANES
    by_pair = pl.BlockSpec((tokens, width), lambda j: (0, j))
    near_specs = [pl.BlockSpec((*x.shape[:2], width), lambda j: (0, 0, j)) for x in nearby]
    totals = pl.BlockSpec((PER_STEP, 8, 2 * tokens), lambda j: (j, 0, 0))
    return by_pair, near_specs, totals, [pl.BlockSpec(x.shape, lambda j: (0, 0)) for x in mask]


def attend(queries, nearby, mask):
    tokens, inner = queries.shape
    keys = mask[0].shape[0]
    by_pair, near_specs, totals, mask_specs = specs(tokens, nearby, mask)
    return pl.pallas_call(
        attend_kernel,
        grid=(inner // LANES // PER_STEP,),
        in_specs=[by_pair, *near_specs, *mask_specs],
        out_specs=[by_pair, totals],
        out_shape=[
            jax.ShapeDtypeStruct((tokens, inner), jnp.bfloat16),
            jax.ShapeDtypeStruct((inner // LANES, 8, 2 * tokens), jnp.float32),
        ],
        cost_estimate=pl.CostEstimate(
            flops=8 * keys * tokens * inner, bytes_accessed=4 * keys * inner,
            transcendentals=keys * tokens * 20),
        name="attend",
    )(queries, *nearby, *mask)


def attention_grads(queries, grads, totals, nearby, mask):
    tokens, inner = queries.shape
    keys = mask[0].shape[0]
    by_pair, near_specs, totals_spec, mask_specs = specs(tokens, nearby, mask)
    return pl.pallas_call(
        grads_kernel,
        grid=(inner // LANES // PER_STEP,),
        in_specs=[by_pair, by_pair, totals_spec, *near_specs, *mask_specs],
        out_specs=[by_pair, *near_specs],
        out_shape=[jax.ShapeDtypeStruct((tokens, inner), jnp.bfloat16)]
        + [jax.ShapeDtypeStruct(x.shape, jnp.bfloat16) for x in nearby],
        cost_estimate=pl.CostEstimate(
            flops=20 * keys * tokens * inner, bytes_accessed=8 * keys * inner,
            transcendentals=keys * tokens * 20),
        name="attention_grads",
    )(queries, grads, totals, *nearby, *mask)


def step(queries, keys, values, grad_out, out_weight, windows):
    frames, row_count, col_count, inner = queries.shape
    model_width = grad_out.shape[3]
    tokens = frames * row_count * col_count
    all_frames = frames * lax.axis_size(TA)
    all_rows = row_count * lax.axis_size(HA)
    total_tokens = all_frames * all_rows * col_count
    flat_queries = queries.reshape(tokens, inner)
    flat_grad = grad_out.reshape(tokens, model_width)

    own = jnp.stack([keys.reshape(tokens, inner), values.reshape(tokens, inner)])
    below = shifted(own[:, tokens - col_count :], HA, 1)
    above = shifted(own[:, :col_count], HA, -1)
    wide = jnp.concatenate([below, own, above], axis=1)
    nearby = (shifted(wide, TA, 1), wide, shifted(wide, TA, -1))

    wide_half = model_width // 2
    odd = lax.axis_index("y") % 2
    from_pair = flipped(
        lax.dynamic_slice_in_dim(flat_grad, (1 - odd) * wide_half, wide_half, axis=1), 1, 0
    )
    mine = lax.dynamic_slice_in_dim(flat_grad, odd * wide_half, wide_half, axis=1)
    mine = jnp.stack([mine, from_pair])
    others = flipped(mine, 0, 1)
    group_grad = jnp.stack([mine, others], axis=1).reshape(4 * tokens, wide_half)

    weight = gathered_weight(out_weight)
    order = row_order(out_weight.shape[0])
    picks = (order[:, None] == lax.broadcasted_iota(jnp.int32, (1, inner), 1)).astype(jnp.bfloat16)
    mask = (
        key_groups(row_count, col_count),
        visible_groups(windows, all_frames, all_rows, row_count, col_count),
    )

    attended, totals = attend(flat_queries, nearby, mask)
    picked = dot(attended, picks, 1, 1).astype(jnp.bfloat16)
    half = inner // 2
    group_attended = jnp.concatenate(
        [picked[:, :half], flipped(picked[:, half:], 0, 1),
         flipped(picked[:, :half], 1, 0), flipped(picked[:, half:], 1, 1)], axis=0
    )
    partial = dot(group_attended, group_grad, 0, 0) * total_tokens ** (-0.5)
    partial = partial.astype(jnp.bfloat16)
    weight_grad = scattered_sum(partial)

    sent = dot(group_grad, weight, 1, 1).astype(jnp.bfloat16)
    here_other = flipped(sent[tokens : 2 * tokens], 0, 1)
    pair_own = flipped(sent[2 * tokens : 3 * tokens], 1, 0)
    pair_other = flipped(sent[3 * tokens :], 1, 1)
    own_half = sent[:tokens].astype(jnp.float32) + pair_own.astype(jnp.float32)
    other_half = here_other.astype(jnp.float32) + pair_other.astype(jnp.float32)
    split_attn = jnp.concatenate([own_half, other_half], axis=1).astype(jnp.bfloat16)
    grad_attn = dot(split_attn, picks, 1, 0).astype(jnp.bfloat16)

    query_grad, before, here, after = attention_grads(flat_queries, grad_attn, totals, nearby, mask)
    before = shifted(before, TA, -1)
    after = shifted(after, TA, 1)
    here = here.astype(jnp.float32) + before.astype(jnp.float32) + after.astype(jnp.float32)
    low = here[:, :col_count].astype(jnp.bfloat16)
    high = here[:, tokens + col_count :].astype(jnp.bfloat16)
    low = shifted(low, HA, -1).astype(jnp.float32)
    high = shifted(high, HA, 1).astype(jnp.float32)
    rest = jnp.zeros_like(here[:, : tokens - col_count])
    total = (here[:, col_count : tokens + col_count] + jnp.concatenate([high, rest], axis=1)
             + jnp.concatenate([rest, low], axis=1)).astype(jnp.bfloat16)
    return (
        query_grad.reshape(queries.shape),
        total[0].reshape(queries.shape),
        total[1].reshape(queries.shape),
        weight_grad,
    )


def solution(mesh):
    fine = Mesh(mesh.devices.reshape(MESH_SHAPE), MESH_NAMES)
    tokens = P(TA, HA, None, None)
    rows = P(TA + HA, None)
    return jax.shard_map(
        step,
        mesh=fine,
        in_specs=(tokens, tokens, tokens, tokens, rows, tokens),
        out_specs=(tokens, tokens, tokens, rows),
        check_vma=False,
    )
```
